32 devices in a mesh: row: 8 (over y, x, core), col: 4 (over z).
Axes of the slice: x: 2, y: 2, z: 4, core: 2. Of those that a mesh axis runs over, the one named last changes fastest.
Arguments:
- pair_slab: float32 [4096, 8000], P(('row', 'col')), may hold values from -0.09375 to 0.09375
- occ_energy: float32 [4], replicated, may hold values from -1 to -0.3
- virt_energy: float32 [1024], replicated, may hold values from 0.1 to 3
Outputs:
- polar: float32 [8000, 8000], P('row', 'col')
The draws below stay inside these ranges and needn't reach their ends.
All inputs are finite; a program needn't handle non-finite values.
Results may differ from the reference program's by a relative error of at most 0.000076.
Values sent between devices are 32-bit elements; how exact they have to be, the bound alone decides.
A program may use at most 192 MiB of HBM per device.

```python
import jax
import jax.numpy as jnp
from jax import lax

NAUX = 8000
NVIRT = 1024
NOCC = 4
NPAIR = 4096


def level_of(own_key, extent, cuts, smallest, high):
    factor_of, own = 1.0, jax.random.fold_in(own_key, 6)
    for position, parts in cuts:
        heights = jnp.exp(jax.random.uniform(jax.random.fold_in(own, position), (parts,), jnp.float32, smallest / len(cuts), high / len(cuts)))
        factor_of = factor_of * jnp.repeat(heights, extent[position] // parts).reshape([-1 if axis == position else 1 for axis in range(len(extent))])
    return factor_of


def gaussian(rng, shape, scale, most, split=(), dtype=jnp.bfloat16):
    factor_of = level_of(rng, shape, split, -0.22, 0.18) if split else 1.0
    entries = jax.random.normal(rng, shape, jnp.float32) * scale * factor_of
    return jnp.minimum(jnp.maximum(entries, -most), most).astype(dtype)


def setup_inputs(seed: int = 0) -> dict:
    seeds = jax.random.split(jax.random.key(seed), 4)
    return {
        "pair_slab": gaussian(seeds[0], (NPAIR, NAUX), NPAIR ** -0.5, 0.09375, ((0, 32),), jnp.float32),
        "occ_energy": jnp.clip(jax.random.uniform(seeds[1], (NOCC,), jnp.float32, -1.0, -0.3), -1.0, -0.3),
        "virt_energy": jnp.clip(jax.random.uniform(seeds[2], (NVIRT,), jnp.float32, 0.1, 3.0), 0.1, 3.0),
    }


def reference(pair_slab, occ_energy, virt_energy):
    gap = (virt_energy[None, :] - occ_energy[:, None]).reshape(-1)
    scaling = 2.0 * gap / (gap * gap + 0.25)
    scaled = pair_slab * scaling[:, None]
    return jnp.dot(scaled.T, pair_slab, precision=lax.Precision.HIGHEST, preferred_element_type=jnp.float32)
```

```python
import functools

import jax
import jax.numpy as jnp
from jax import lax
from jax.experimental import pallas as pl
from jax.experimental.pallas import tpu as pltpu
from jax.sharding import PartitionSpec as P

MESH = pl.DeviceIdType.MESH
TILE = 256


def scaling_of(occ_energy, virt_energy):
    gap = (virt_energy[None, :] - occ_energy[:, None]).reshape(-1)
    return 2.0 * gap / (gap * gap + 0.25)


def padded(width, to):
    return -(-width // to) * to


def kernel(R, Z, S, x_ref, y_ref, out_ref, left, right, acc, lbuf, rbuf, lhi, llo,
           recv_l, recv_r, s_a, s_b, s_up, s_dn, s_c, s_relay, s_load):
    r = lax.axis_index("row")
    z = lax.axis_index("col")
    par = lax.rem(r, 2)
    sib = r + 1 - 2 * par
    half = R // 2

    def slot_of(ref, zz, rr):
        return ref.at[zz, rr // 2, pl.ds(lax.rem(rr, 2) * S, S)]

    def wait(ref, sem):
        pltpu.make_async_copy(ref, ref, sem).wait()

    def send(src, dst, send_sem, recv_sem, rr, zz):
        pltpu.make_async_remote_copy(
            src_ref=src, dst_ref=dst, send_sem=send_sem, recv_sem=recv_sem,
            device_id=(rr, zz), device_id_type=MESH,
        ).start()

    def loop(n, body):
        def step(i, carry):
            body(i)
            return carry
        lax.fori_loop(0, n, step, 0)

    barrier = pltpu.get_barrier_semaphore()

    def greet_row(i):
        pl.semaphore_signal(barrier, inc=1, device_id=(lax.rem(r + 1 + i, R), z), device_id_type=MESH)

    def greet_col(i):
        pl.semaphore_signal(barrier, inc=1, device_id=(r, lax.rem(z + 1 + i, Z)), device_id_type=MESH)

    loop(R - 1, greet_row)
    loop(Z - 1, greet_col)
    pl.semaphore_wait(barrier, R - 1 + Z - 1)

    def spread_right(src, zz):
        def to_peer(i):
            rr = lax.rem(r + 2 * (i + 1), R)
            send(src, slot_of(right, zz, r), s_c.at[zz, rr], recv_r.at[zz, r], rr, z)
        send(src, slot_of(right, zz, r), s_c.at[zz, sib], recv_r.at[zz, r], sib, z)
        loop(half - 1, to_peer)

    def a2a_right(i):
        zz = lax.rem(z + 1 + i, Z)
        send(y_ref.at[zz], slot_of(right, z, r), s_a.at[zz], recv_r.at[z, r], r, zz)

    def a2a_left(i):
        rr = lax.rem(r + 1 + i, R)
        send(x_ref.at[rr], slot_of(left, z, r), s_b.at[rr], recv_l.at[z, r], rr, z)

    pltpu.make_async_copy(x_ref.at[r], slot_of(left, z, r), recv_l.at[z, r]).start()
    pltpu.make_async_copy(y_ref.at[z], slot_of(right, z, r), recv_r.at[z, r]).start()
    loop(Z - 1, a2a_right)
    loop(R - 1, a2a_left)
    spread_right(y_ref.at[z], z)
    wait(slot_of(right, z, r), recv_r.at[z, r])
    acc[...] = jnp.zeros_like(acc)

    def goes_up(zz):
        return jnp.logical_and(zz <= z, z < Z - 1)

    def goes_down(zz):
        return jnp.logical_and(zz >= z, z > 0)

    def forward(zz, p):
        @pl.when(jnp.logical_or(goes_up(zz), goes_down(zz)))
        def _():
            def one(h):
                rr = 2 * p + h
                block = slot_of(left, zz, rr)
                wait(block, recv_l.at[zz, rr])

                @pl.when(goes_up(zz))
                def _():
                    send(block, block, s_up.at[zz, rr], recv_l.at[zz, rr], r, z + 1)

                @pl.when(goes_down(zz))
                def _():
                    send(block, block, s_dn.at[zz, rr], recv_l.at[zz, rr], r, z - 1)
            loop(2, one)

    def compute(zz, p):
        mine = 2 * p + par
        other = 2 * p + 1 - par
        block = slot_of(right, zz, mine)

        @pl.when(mine != r)
        def _():
            wait(block, recv_r.at[zz, mine])
            send(block, block, s_relay.at[zz, mine], recv_r.at[zz, mine], sib, z)

        @pl.when(jnp.logical_not(jnp.logical_or(goes_up(zz), goes_down(zz))))
        def _():
            def one(h):
                wait(slot_of(left, zz, 2 * p + h), recv_l.at[zz, 2 * p + h])
            loop(2, one)

        wait(slot_of(right, zz, other), recv_r.at[zz, other])
        load_l = pltpu.make_async_copy(left.at[zz, p], lbuf, s_load.at[0])
        load_r = pltpu.make_async_copy(right.at[zz, p], rbuf, s_load.at[1])
        load_l.start()
        load_r.start()
        load_l.wait()
        turned = lbuf[...].T
        top = turned.astype(jnp.bfloat16)
        lhi[...] = top
        llo[...] = (turned - top.astype(jnp.float32)).astype(jnp.bfloat16)
        load_r.wait()

        def column(t):
            cols = pl.ds(pl.multiple_of(t * TILE, TILE), TILE)
            b = rbuf[:, cols]
            bhi = b.astype(jnp.bfloat16)
            blo = (b - bhi.astype(jnp.float32)).astype(jnp.bfloat16)
            dot = functools.partial(jnp.dot, preferred_element_type=jnp.float32)
            acc[:, cols] += dot(lhi[...], bhi) + (dot(lhi[...], blo) + dot(llo[...], bhi))
        loop(acc.shape[1] // TILE, column)

    def both(d, do):
        @pl.when(z - d >= 0)
        def _():
            do(z - d)

        @pl.when(jnp.logical_and(d > 0, z + d < Z))
        def _():
            do(z + d)

    loop(half, lambda p: forward(z, p))

    def gathered(d):
        def one(zz):
            wait(slot_of(right, zz, r), recv_r.at[zz, r])
            spread_right(slot_of(right, zz, r), zz)
        both(d + 1, one)
    loop(Z - 1, gathered)

    def stage(s):
        def step(p):
            @pl.when(s + 1 < Z)
            def _():
                both(s + 1, lambda zz: forward(zz, p))
            both(s, lambda zz: compute(zz, p))
        loop(half, step)
    loop(Z, stage)

    write = pltpu.make_async_copy(acc, out_ref, s_load.at[0])
    write.start()

    def drain_a(i):
        zz = lax.rem(z + 1 + i, Z)
        wait(y_ref.at[zz], s_a.at[zz])

    def drain_b(i):
        rr = lax.rem(r + 1 + i, R)
        wait(x_ref.at[rr], s_b.at[rr])

    loop(Z - 1, drain_a)
    loop(R - 1, drain_b)

    def drain(zz):
        wait(slot_of(right, zz, r), s_c.at[zz, sib])

        def to_peer(i):
            rr = lax.rem(r + 2 * (i + 1), R)
            wait(slot_of(right, zz, r), s_c.at[zz, rr])
            wait(slot_of(right, zz, rr), s_relay.at[zz, rr])
        loop(half - 1, to_peer)

        def line(rr):
            @pl.when(goes_up(zz))
            def _():
                wait(slot_of(left, zz, rr), s_up.at[zz, rr])

            @pl.when(goes_down(zz))
            def _():
                wait(slot_of(left, zz, rr), s_dn.at[zz, rr])
        loop(R, line)
    loop(Z, drain)
    write.wait()


def local(pair_slab, occ_energy, virt_energy):
    R = lax.axis_size("row")
    Z = lax.axis_size("col")
    S, naux = pair_slab.shape
    wl, wr = naux // R, naux // Z
    pl_, pr_ = padded(wl, 128), padded(wr, TILE)
    me = lax.axis_index("row") * Z + lax.axis_index("col")
    scaling = lax.dynamic_slice(scaling_of(occ_energy, virt_energy), (me * S,), (S,))
    scaled = pair_slab * scaling[:, None]
    x = jnp.stack([jnp.pad(pair_slab[:, i * wl:(i + 1) * wl], ((0, 0), (0, pl_ - wl))) for i in range(R)])
    y = jnp.stack([jnp.pad(scaled[:, i * wr:(i + 1) * wr], ((0, 0), (0, pr_ - wr))) for i in range(Z)])
    anyspace = pl.BlockSpec(memory_space=pl.ANY)
    dma = pltpu.SemaphoreType.DMA
    out = pl.pallas_call(
        functools.partial(kernel, R, Z, S),
        out_shape=(
            jax.ShapeDtypeStruct((pl_, pr_), jnp.float32),
            jax.ShapeDtypeStruct((Z, R // 2, 2 * S, pl_), jnp.float32),
            jax.ShapeDtypeStruct((Z, R // 2, 2 * S, pr_), jnp.float32),
        ),
        in_specs=[anyspace] * 2,
        out_specs=(anyspace,) * 3,
        scratch_shapes=[
            pltpu.VMEM((pl_, pr_), jnp.float32),
            pltpu.VMEM((2 * S, pl_), jnp.float32),
            pltpu.VMEM((2 * S, pr_), jnp.float32),
            pltpu.VMEM((pl_, 2 * S), jnp.bfloat16),
            pltpu.VMEM((pl_, 2 * S), jnp.bfloat16),
            dma((Z, R)), dma((Z, R)),
            dma((Z,)), dma((R,)), dma((Z, R)), dma((Z, R)), dma((Z, R)), dma((Z, R)), dma((2,)),
        ],
        compiler_params=pltpu.CompilerParams(
            collective_id=0, has_side_effects=True, vmem_limit_bytes=56 * 2**20
        ),
    )(x, y)[0]
    return out[:wl, :wr]


def solution(mesh):
    in_specs = (P(("row", "col"), None), P(), P())
    out_specs = P("row", "col")
    return jax.shard_map(local, mesh=mesh, in_specs=in_specs, out_specs=out_specs, check_vma=False)
```

```python
import functools

import jax
import jax.numpy as jnp
from jax import lax
from jax.experimental import pallas as pl
from jax.experimental.pallas import tpu as pltpu
from jax.sharding import PartitionSpec as P

MESH = pl.DeviceIdType.MESH
TILE = 256


def scaling_of(occ_energy, virt_energy):
    gap = (virt_energy[None, :] - occ_energy[:, None]).reshape(-1)
    return 2.0 * gap / (gap * gap + 0.25)


def kernel(R, Z, S, x_ref, y_ref, scal_ref, out_ref, left, right, acc, lbuf, rbuf, lhi, llo,
           recv_l, recv_r, s_a, s_b, s_up, s_dn, s_c, s_relay, s_load):
    r = lax.axis_index("row")
    z = lax.axis_index("col")
    par = lax.rem(r, 2)
    sib = r + 1 - 2 * par
    half = R // 2

    def slot_of(ref, zz, rr):
        return ref.at[zz, rr]

    def wait(ref, sem):
        pltpu.make_async_copy(ref, ref, sem).wait()

    def send(src, dst, send_sem, recv_sem, rr, zz):
        pltpu.make_async_remote_copy(
            src_ref=src, dst_ref=dst, send_sem=send_sem, recv_sem=recv_sem,
            device_id=(rr, zz), device_id_type=MESH,
        ).start()

    def loop(n, body):
        def step(i, carry):
            body(i)
            return carry
        lax.fori_loop(0, n, step, 0)

    barrier = pltpu.get_barrier_semaphore()

    def greet_row(i):
        pl.semaphore_signal(barrier, inc=1, device_id=(lax.rem(r + 1 + i, R), z), device_id_type=MESH)

    def greet_col(i):
        pl.semaphore_signal(barrier, inc=1, device_id=(r, lax.rem(z + 1 + i, Z)), device_id_type=MESH)

    loop(R - 1, greet_row)
    loop(Z - 1, greet_col)
    pl.semaphore_wait(barrier, R - 1 + Z - 1)

    def spread_right(src, zz):
        def to_peer(i):
            rr = lax.rem(r + 2 * (i + 1), R)
            send(src, slot_of(right, zz, r), s_c.at[zz, rr], recv_r.at[zz, r], rr, z)
        send(src, slot_of(right, zz, r), s_c.at[zz, sib], recv_r.at[zz, r], sib, z)
        loop(half - 1, to_peer)

    def a2a_right(i):
        zz = lax.rem(z + 1 + i, Z)
        send(y_ref.at[zz], slot_of(right, z, r), s_a.at[zz], recv_r.at[z, r], r, zz)

    def a2a_left(i):
        rr = lax.rem(r + 1 + i, R)
        send(x_ref.at[rr], slot_of(left, z, r), s_b.at[rr], recv_l.at[z, r], rr, z)

    pltpu.make_async_copy(x_ref.at[r], slot_of(left, z, r), recv_l.at[z, r]).start()
    pltpu.make_async_copy(y_ref.at[z], slot_of(right, z, r), recv_r.at[z, r]).start()
    loop(Z - 1, a2a_right)
    loop(R - 1, a2a_left)
    spread_right(y_ref.at[z], z)
    wait(slot_of(right, z, r), recv_r.at[z, r])
    acc[...] = jnp.zeros_like(acc)

    def goes_up(zz):
        return jnp.logical_and(zz <= z, z < Z - 1)

    def goes_down(zz):
        return jnp.logical_and(zz >= z, z > 0)

    def forward(zz, p):
        @pl.when(jnp.logical_or(goes_up(zz), goes_down(zz)))
        def _():
            def one(h):
                rr = 2 * p + h
                block = slot_of(left, zz, rr)
                wait(block, recv_l.at[zz, rr])

                @pl.when(goes_up(zz))
                def _():
                    send(block, block, s_up.at[zz, rr], recv_l.at[zz, rr], r, z + 1)

                @pl.when(goes_down(zz))
                def _():
                    send(block, block, s_dn.at[zz, rr], recv_l.at[zz, rr], r, z - 1)
            loop(2, one)

    def compute(zz, p):
        mine = 2 * p + par
        other = 2 * p + 1 - par
        block = slot_of(right, zz, mine)

        @pl.when(mine != r)
        def _():
            wait(block, recv_r.at[zz, mine])
            send(block, block, s_relay.at[zz, mine], recv_r.at[zz, mine], sib, z)

        @pl.when(jnp.logical_not(jnp.logical_or(goes_up(zz), goes_down(zz))))
        def _():
            def one(h):
                wait(slot_of(left, zz, 2 * p + h), recv_l.at[zz, 2 * p + h])
            loop(2, one)

        wait(slot_of(right, zz, other), recv_r.at[zz, other])
        loads = []
        for h in range(2):
            loads.append(pltpu.make_async_copy(left.at[zz, 2 * p + h], lbuf.at[h], s_load.at[h]))
            loads.append(pltpu.make_async_copy(right.at[zz, 2 * p + h], rbuf.at[h], s_load.at[2 + h]))
        for load in loads:
            load.start()
        for load in loads:
            load.wait()
        a = jnp.concatenate([lbuf[0], lbuf[1]], axis=1) * scal_ref[zz * half + p]
        top = a.astype(jnp.bfloat16)
        lhi[...] = top
        llo[...] = (a - top.astype(jnp.float32)).astype(jnp.bfloat16)

        def product(rows):
            b = jnp.concatenate([rbuf[0, rows], rbuf[1, rows]], axis=1)
            bhi = b.astype(jnp.bfloat16)
            blo = (b - bhi.astype(jnp.float32)).astype(jnp.bfloat16)

            def dot(left_part, right_part):
                return lax.dot_general(
                    left_part, right_part, (((1,), (1,)), ((), ())),
                    preferred_element_type=jnp.float32,
                )
            acc[:, rows] += dot(lhi[...], bhi) + (dot(lhi[...], blo) + dot(llo[...], bhi))

        width = acc.shape[1]
        tiles = width // TILE
        loop(tiles, lambda t: product(pl.ds(pl.multiple_of(t * TILE, TILE), TILE)))
        if width % TILE:
            product(pl.ds(tiles * TILE, width % TILE))

    def both(d, do):
        @pl.when(z - d >= 0)
        def _():
            do(z - d)

        @pl.when(jnp.logical_and(d > 0, z + d < Z))
        def _():
            do(z + d)

    loop(half, lambda p: forward(z, p))

    def gathered(d):
        def one(zz):
            wait(slot_of(right, zz, r), recv_r.at[zz, r])
            spread_right(slot_of(right, zz, r), zz)
        both(d + 1, one)
    loop(Z - 1, gathered)

    def stage(s):
        def step(p):
            @pl.when(s + 1 < Z)
            def _():
                both(s + 1, lambda zz: forward(zz, p))
            both(s, lambda zz: compute(zz, p))
        loop(half, step)
    loop(Z, stage)

    write = pltpu.make_async_copy(acc, out_ref, s_load.at[0])
    write.start()

    def drain_a(i):
        zz = lax.rem(z + 1 + i, Z)
        wait(y_ref.at[zz], s_a.at[zz])

    def drain_b(i):
        rr = lax.rem(r + 1 + i, R)
        wait(x_ref.at[rr], s_b.at[rr])

    loop(Z - 1, drain_a)
    loop(R - 1, drain_b)

    def drain(zz):
        wait(slot_of(right, zz, r), s_c.at[zz, sib])

        def to_peer(i):
            rr = lax.rem(r + 2 * (i + 1), R)
            wait(slot_of(right, zz, r), s_c.at[zz, rr])
            wait(slot_of(right, zz, rr), s_relay.at[zz, rr])
        loop(half - 1, to_peer)

        def line(rr):
            @pl.when(goes_up(zz))
            def _():
                wait(slot_of(left, zz, rr), s_up.at[zz, rr])

            @pl.when(goes_down(zz))
            def _():
                wait(slot_of(left, zz, rr), s_dn.at[zz, rr])
        loop(R, line)
    loop(Z, drain)
    write.wait()


def local(pair_slab, occ_energy, virt_energy):
    R = lax.axis_size("row")
    Z = lax.axis_size("col")
    S, naux = pair_slab.shape
    wl, wr = naux // R, naux // Z
    scaling = scaling_of(occ_energy, virt_energy).reshape(R, Z, S).transpose(1, 0, 2)
    turned = pair_slab.T
    anyspace = pl.BlockSpec(memory_space=pl.ANY)
    dma = pltpu.SemaphoreType.DMA
    return pl.pallas_call(
        functools.partial(kernel, R, Z, S),
        out_shape=(
            jax.ShapeDtypeStruct((wl, wr), jnp.float32),
            jax.ShapeDtypeStruct((Z, R, wl, S), jnp.float32),
            jax.ShapeDtypeStruct((Z, R, wr, S), jnp.float32),
        ),
        in_specs=[anyspace] * 2 + [pl.BlockSpec(memory_space=pltpu.VMEM)],
        out_specs=(anyspace,) * 3,
        scratch_shapes=[
            pltpu.VMEM((wl, wr), jnp.float32),
            pltpu.VMEM((2, wl, S), jnp.float32),
            pltpu.VMEM((2, wr, S), jnp.float32),
            pltpu.VMEM((wl, 2 * S), jnp.bfloat16),
            pltpu.VMEM((wl, 2 * S), jnp.bfloat16),
            dma((Z, R)), dma((Z, R)),
            dma((Z,)), dma((R,)), dma((Z, R)), dma((Z, R)), dma((Z, R)), dma((Z, R)), dma((4,)),
        ],
        compiler_params=pltpu.CompilerParams(
            collective_id=0, has_side_effects=True, vmem_limit_bytes=56 * 2**20
        ),
    )(
        turned.reshape(R, wl, S),
        turned.reshape(Z, wr, S),
        scaling.reshape(Z * (R // 2), 1, 2 * S),
    )[0]


def solution(mesh):
    in_specs = (P(("row", "col"), None), P(), P())
    out_specs = P("row", "col")
    return jax.shard_map(local, mesh=mesh, in_specs=in_specs, out_specs=out_specs, check_vma=False)
```

```python
import functools

import jax
import jax.numpy as jnp
from jax import lax
from jax.experimental import pallas as pl
from jax.experimental.pallas import tpu as pltpu
from jax.sharding import PartitionSpec as P

MESH = pl.DeviceIdType.MESH
TILE = 256


def scaling_of(occ_energy, virt_energy):
    gap = (virt_energy[None, :] - occ_energy[:, None]).reshape(-1)
    return 2.0 * gap / (gap * gap + 0.25)


def split(a):
    top = a.astype(jnp.bfloat16)
    return top, (a - top.astype(jnp.float32)).astype(jnp.bfloat16)


def product(lhi, llo, b):
    bhi, blo = split(b)

    def dot(left_part, right_part):
        return lax.dot_general(
            left_part, right_part, (((1,), (1,)), ((), ())), preferred_element_type=jnp.float32
        )
    return dot(lhi, bhi) + (dot(lhi, blo) + dot(llo, bhi))


def last_kernel(far_ref, acc_ref, left_ref, right_ref, scal_ref, out_ref, lhi, llo):
    @pl.when(pl.program_id(0) == 0)
    def _():
        a = jnp.concatenate([left_ref[0, 0], left_ref[0, 1]], axis=1) * scal_ref[0]
        lhi[...], llo[...] = split(a)
    b = jnp.concatenate([right_ref[0, 0], right_ref[0, 1]], axis=1)
    out_ref[...] = acc_ref[...] + product(lhi[...], llo[...], b)


def kernel(R, Z, S, x_ref, y_ref, scal_ref, out_ref, left, right, acc, lbuf, rbuf, lhi, llo,
           recv_l, recv_r, s_a, s_b, s_up, s_dn, s_c, s_relay, s_load):
    r = lax.axis_index("row")
    z = lax.axis_index("col")
    par = lax.rem(r, 2)
    sib = r + 1 - 2 * par
    half = R // 2

    def slot_of(ref, zz, rr):
        return ref.at[zz, rr]

    def wait(ref, sem):
        pltpu.make_async_copy(ref, ref, sem).wait()

    def send(src, dst, send_sem, recv_sem, rr, zz):
        pltpu.make_async_remote_copy(
            src_ref=src, dst_ref=dst, send_sem=send_sem, recv_sem=recv_sem,
            device_id=(rr, zz), device_id_type=MESH,
        ).start()

    def loop(n, body):
        def step(i, carry):
            body(i)
            return carry
        lax.fori_loop(0, n, step, 0)

    barrier = pltpu.get_barrier_semaphore()

    def greet_row(i):
        pl.semaphore_signal(barrier, inc=1, device_id=(lax.rem(r + 1 + i, R), z), device_id_type=MESH)

    def greet_col(i):
        pl.semaphore_signal(barrier, inc=1, device_id=(r, lax.rem(z + 1 + i, Z)), device_id_type=MESH)

    loop(R - 1, greet_row)
    loop(Z - 1, greet_col)
    pl.semaphore_wait(barrier, R - 1 + Z - 1)

    def spread_right(src, zz):
        def to_peer(i):
            rr = lax.rem(r + 2 * (i + 1), R)
            send(src, slot_of(right, zz, r), s_c.at[zz, rr], recv_r.at[zz, r], rr, z)
        send(src, slot_of(right, zz, r), s_c.at[zz, sib], recv_r.at[zz, r], sib, z)
        loop(half - 1, to_peer)

    def a2a_right(i):
        zz = lax.rem(z + 1 + i, Z)
        send(y_ref.at[zz], slot_of(right, z, r), s_a.at[zz], recv_r.at[z, r], r, zz)

    def a2a_left(i):
        rr = lax.rem(r + 1 + i, R)
        send(x_ref.at[rr], slot_of(left, z, r), s_b.at[rr], recv_l.at[z, r], rr, z)

    pltpu.make_async_copy(x_ref.at[r], slot_of(left, z, r), recv_l.at[z, r]).start()
    pltpu.make_async_copy(y_ref.at[z], slot_of(right, z, r), recv_r.at[z, r]).start()
    loop(Z - 1, a2a_right)
    loop(R - 1, a2a_left)
    spread_right(y_ref.at[z], z)
    wait(slot_of(right, z, r), recv_r.at[z, r])
    acc[...] = jnp.zeros_like(acc)

    def goes_up(zz):
        return jnp.logical_and(zz <= z, z < Z - 1)

    def goes_down(zz):
        return jnp.logical_and(zz >= z, z > 0)

    def forward(zz, p):
        @pl.when(jnp.logical_or(goes_up(zz), goes_down(zz)))
        def _():
            def one(h):
                rr = 2 * p + h
                block = slot_of(left, zz, rr)
                wait(block, recv_l.at[zz, rr])

                @pl.when(goes_up(zz))
                def _():
                    send(block, block, s_up.at[zz, rr], recv_l.at[zz, rr], r, z + 1)

                @pl.when(goes_down(zz))
                def _():
                    send(block, block, s_dn.at[zz, rr], recv_l.at[zz, rr], r, z - 1)
            loop(2, one)

    def multiply(zz, p):
        loads = []
        for h in range(2):
            loads.append(pltpu.make_async_copy(left.at[zz, 2 * p + h], lbuf.at[h], s_load.at[h]))
            loads.append(pltpu.make_async_copy(right.at[zz, 2 * p + h], rbuf.at[h], s_load.at[2 + h]))
        for load in loads:
            load.start()
        for load in loads:
            load.wait()
        a = jnp.concatenate([lbuf[0], lbuf[1]], axis=1) * scal_ref[zz * half + p]
        lhi[...], llo[...] = split(a)

        def columns(rows):
            b = jnp.concatenate([rbuf[0, rows], rbuf[1, rows]], axis=1)
            acc[:, rows] += product(lhi[...], llo[...], b)

        width = acc.shape[1]
        tiles = width // TILE
        loop(tiles, lambda t: columns(pl.ds(pl.multiple_of(t * TILE, TILE), TILE)))
        if width % TILE:
            columns(pl.ds(tiles * TILE, width % TILE))

    far = jnp.where(Z - 1 - z >= z, Z - 1, 0)
    write = pltpu.make_async_copy(acc, out_ref, s_load.at[0])

    def compute(zz, p):
        last = jnp.logical_and(zz == far, p == half - 1)

        @pl.when(last)
        def _():
            write.start()

        mine = 2 * p + par
        other = 2 * p + 1 - par
        block = slot_of(right, zz, mine)

        @pl.when(mine != r)
        def _():
            wait(block, recv_r.at[zz, mine])
            send(block, block, s_relay.at[zz, mine], recv_r.at[zz, mine], sib, z)

        @pl.when(jnp.logical_not(jnp.logical_or(goes_up(zz), goes_down(zz))))
        def _():
            def one(h):
                wait(slot_of(left, zz, 2 * p + h), recv_l.at[zz, 2 * p + h])
            loop(2, one)

        wait(slot_of(right, zz, other), recv_r.at[zz, other])
        @pl.when(jnp.logical_not(last))
        def _():
            multiply(zz, p)

    def both(d, do):
        @pl.when(z - d >= 0)
        def _():
            do(z - d)

        @pl.when(jnp.logical_and(d > 0, z + d < Z))
        def _():
            do(z + d)

    loop(half, lambda p: forward(z, p))

    def gathered(d):
        def one(zz):
            wait(slot_of(right, zz, r), recv_r.at[zz, r])
            spread_right(slot_of(right, zz, r), zz)
        both(d + 1, one)
    loop(Z - 1, gathered)

    def stage(s):
        def step(p):
            @pl.when(s + 1 < Z)
            def _():
                both(s + 1, lambda zz: forward(zz, p))
            both(s, lambda zz: compute(zz, p))
        loop(half, step)
    loop(Z, stage)

    def drain_a(i):
        zz = lax.rem(z + 1 + i, Z)
        wait(y_ref.at[zz], s_a.at[zz])

    def drain_b(i):
        rr = lax.rem(r + 1 + i, R)
        wait(x_ref.at[rr], s_b.at[rr])

    loop(Z - 1, drain_a)
    loop(R - 1, drain_b)

    def drain(zz):
        wait(slot_of(right, zz, r), s_c.at[zz, sib])

        def to_peer(i):
            rr = lax.rem(r + 2 * (i + 1), R)
            wait(slot_of(right, zz, r), s_c.at[zz, rr])
            wait(slot_of(right, zz, rr), s_relay.at[zz, rr])
        loop(half - 1, to_peer)

        def line(rr):
            @pl.when(goes_up(zz))
            def _():
                wait(slot_of(left, zz, rr), s_up.at[zz, rr])

            @pl.when(goes_down(zz))
            def _():
                wait(slot_of(left, zz, rr), s_dn.at[zz, rr])
        loop(R, line)
    loop(Z, drain)
    write.wait()


def local(pair_slab, occ_energy, virt_energy):
    R = lax.axis_size("row")
    Z = lax.axis_size("col")
    S, naux = pair_slab.shape
    wl, wr = naux // R, naux // Z
    scaling = scaling_of(occ_energy, virt_energy).reshape(R, Z, S).transpose(1, 0, 2)
    turned = pair_slab.T
    anyspace = pl.BlockSpec(memory_space=pl.ANY)
    dma = pltpu.SemaphoreType.DMA
    scal = scaling.reshape(Z * (R // 2), 1, 2 * S)
    acc, left, right = pl.pallas_call(
        functools.partial(kernel, R, Z, S),
        out_shape=(
            jax.ShapeDtypeStruct((wl, wr), jnp.float32),
            jax.ShapeDtypeStruct((Z, R, wl, S), jnp.float32),
            jax.ShapeDtypeStruct((Z, R, wr, S), jnp.float32),
        ),
        in_specs=[anyspace] * 2 + [pl.BlockSpec(memory_space=pltpu.VMEM)],
        out_specs=(anyspace,) * 3,
        scratch_shapes=[
            pltpu.VMEM((wl, wr), jnp.float32),
            pltpu.VMEM((2, wl, S), jnp.float32),
            pltpu.VMEM((2, wr, S), jnp.float32),
            pltpu.VMEM((wl, 2 * S), jnp.bfloat16),
            pltpu.VMEM((wl, 2 * S), jnp.bfloat16),
            dma((Z, R)), dma((Z, R)),
            dma((Z,)), dma((R,)), dma((Z, R)), dma((Z, R)), dma((Z, R)), dma((Z, R)), dma((4,)),
        ],
        compiler_params=pltpu.CompilerParams(
            collective_id=0, has_side_effects=True, vmem_limit_bytes=56 * 2**20
        ),
    )(
        turned.reshape(R, wl, S),
        turned.reshape(Z, wr, S),
        scal,
    )
    z = lax.axis_index("col")
    half = R // 2
    far = jnp.where(Z - 1 - z >= z, Z - 1, 0).astype(jnp.int32).reshape(1)
    return pl.pallas_call(
        last_kernel,
        out_shape=jax.ShapeDtypeStruct((wl, wr), jnp.float32),
        grid_spec=pltpu.PrefetchScalarGridSpec(
            num_scalar_prefetch=1,
            grid=(pl.cdiv(wr, TILE),),
            in_specs=[
                pl.BlockSpec((wl, TILE), lambda t, f: (0, t)),
                pl.BlockSpec((1, 2, wl, S), lambda t, f: (f[0], half - 1, 0, 0)),
                pl.BlockSpec((1, 2, TILE, S), lambda t, f: (f[0], half - 1, t, 0)),
                pl.BlockSpec((1, 1, 2 * S), lambda t, f: (f[0] * half + half - 1, 0, 0)),
            ],
            out_specs=pl.BlockSpec((wl, TILE), lambda t, f: (0, t)),
            scratch_shapes=[
                pltpu.VMEM((wl, 2 * S), jnp.bfloat16),
                pltpu.VMEM((wl, 2 * S), jnp.bfloat16),
            ],
        ),
    )(far, acc, left, right, scal)


def solution(mesh):
    in_specs = (P(("row", "col"), None), P(), P())
    out_specs = P("row", "col")
    return jax.shard_map(local, mesh=mesh, in_specs=in_specs, out_specs=out_specs, check_vma=False)
```
